32 devices in a mesh: rep: 8 (over z, x), shard: 4 (over y, core).
Axes of the slice: x: 2, y: 2, z: 4, core: 2. Of those that a mesh axis runs over, the one named last changes fastest.
Arguments:
- inputs: bfloat16 [3072, 1024], P('rep', 'shard'), may hold values from -6 to 6
- cotangent: bfloat16 [3072, 512], P('rep'), may hold values from -0.15625 to 0.15625
- momentum: float32 [512, 1024], P('rep', 'shard'), may hold values from -54 to 54
- right_prev: float32 [1024, 64], P('shard'), may hold values from -0.1875 to 0.1875
Outputs:
- new_momentum: float32 [512, 1024], P('rep', 'shard')
- right_factor: float32 [1024, 64], P('shard')
- update: bfloat16 [512, 1024], P('rep', 'shard')
The draws below stay inside these ranges and needn't reach their ends.
All inputs are finite; a program needn't handle non-finite values.
Results may differ from the reference program's by a relative error of at most 0.001.
Values sent between devices are 32-bit elements; how exact they have to be, the bound alone decides.
A program may use at most 64 MiB of HBM per device.

```python
import math
import jax
import jax.numpy as jnp
from jax import lax

R = 64
OUT = 512
IN = 1024
TOKENS = 3072


def draw_momentum(key, part):
    first_key, second_key = jax.random.split(key, 2)
    position = jnp.arange(OUT, dtype=jnp.float32) / max(OUT - 1, 1)
    ramp_scale = 1.0 + 2.0 * position
    row_scale = jnp.exp(jax.random.uniform(second_key, (OUT, 1), jnp.float32, math.log(0.3), math.log(3.0)))
    base_draw = jax.random.normal(first_key, (OUT, IN), jnp.float32)
    base_draw = jnp.clip(base_draw, -6.0, 6.0)
    return base_draw * row_scale * ramp_scale[:, None]


def raised(entries, rng, source, target, parts, factor):
    owner, partner = [(jnp.arange(entries.shape[dim]) // (entries.shape[dim] // parts)).reshape([-1 if axis == dim else 1 for axis in range(entries.ndim)]) for dim in (source, target)]
    chosen = jax.random.permutation(rng, parts)[partner]
    strong = (owner == chosen) | (owner == (partner + parts // 2) % parts)
    return jnp.where(strong, factor * entries, entries)


def block_levels(own_key, dims, cuts, least, top_value):
    def one(axis_at, blocks):
        heights = jax.random.uniform(jax.random.fold_in(jax.random.fold_in(own_key, 6), axis_at), (blocks,), jnp.float32, least / len(cuts), top_value / len(cuts))
        return jnp.repeat(jnp.exp(heights), dims[axis_at] // blocks).reshape((-1,) + (1,) * (len(dims) - axis_at - 1))

    loudness = one(*cuts[0])
    for cut in cuts[1:]:
        loudness = loudness * one(*cut)
    return loudness


def noise(rng, dims, scale, reach, pieces=(), kind=jnp.bfloat16):
    values = jax.random.normal(rng, dims, jnp.float32) * scale
    if len(pieces) > 0:
        values = block_levels(rng, dims, pieces, -0.22, 0.18) * values
    return jnp.clip(values, min=-reach, max=reach).astype(kind)


def bell_draw_with(stream_key, extent, deviation, reach, pieces, heavy, kind=jnp.bfloat16):
    drawn = deviation * jax.random.normal(stream_key, extent, jnp.float32)
    if pieces:
        drawn = drawn * block_levels(stream_key, extent, pieces, -0.22, 0.18)
    return jnp.clip(raised(drawn, jax.random.fold_in(stream_key, 3), *heavy), -reach, reach).astype(kind)


def setup_inputs(seed: int = 0) -> dict:
    streams_of = jax.random.split(jax.random.key(seed), 5)
    inputs = noise(streams_of[0], (TOKENS, IN), 1.0, 6.0, ((0, 8), (1, 4)))
    cotangent = bell_draw_with(streams_of[1], (TOKENS, OUT), TOKENS ** -0.5, 0.15625, ((0, 8),), (0, 1, 8, 2.0))
    momentum = draw_momentum(jax.random.fold_in(streams_of[4], 71), 0)
    right_prev = noise(streams_of[3], (IN, R), IN ** -0.5, 0.1875, ((0, 4),), jnp.float32)
    return {"inputs": inputs, "cotangent": cotangent, "momentum": momentum, "right_prev": right_prev}


def reference(inputs, cotangent, momentum, right_prev):
    high = lax.Precision.HIGHEST
    gradient = lax.dot_general(cotangent.astype(jnp.float32), inputs.astype(jnp.float32), (((0,), (0,)), ((), ())), precision=high, preferred_element_type=jnp.float32)
    blended = momentum + gradient
    left_raw = jnp.dot(blended, right_prev, precision=high)
    gram_sum = jnp.dot(left_raw.T, left_raw, precision=high)
    lower_factor = jnp.linalg.cholesky(gram_sum)
    ortho = lax.linalg.triangular_solve(lower_factor, left_raw.T, left_side=True, lower=True).T
    right_raw = jnp.dot(blended.T, ortho, precision=high)
    new_momentum = blended - 0.05 * jnp.dot(ortho, right_raw.T, precision=high)
    column_sq = lax.optimization_barrier(jnp.sum(right_raw * right_raw, axis=0))
    right_factor = right_raw / jnp.sqrt(column_sq + 1e-06)
    scale_factor = (OUT * IN / R) ** 0.5
    update = (scale_factor * jnp.dot(ortho, right_factor.T, precision=high)).astype(jnp.bfloat16)
    return (new_momentum, right_factor, update)
```

```python
import functools

import jax
import jax.numpy as jnp
from jax import lax
from jax.experimental import pallas as pl
from jax.experimental.pallas import tpu as pltpu
from jax.sharding import PartitionSpec as P

MESH = pl.DeviceIdType.MESH
F32, BF16 = jnp.float32, jnp.bfloat16
SUB, LANE = 8, 128
NT = (((1,), (1,)), ((), ()))
NN = (((1,), (0,)), ((), ()))
TN = (((0,), (0,)), ((), ()))


def split(x):
    hi = x.astype(BF16)
    lo = (x - hi.astype(F32)).astype(BF16)
    return jnp.concatenate([hi, lo], axis=0)


def dot_split(x, y, dims):
    rows = x.shape[0]
    both = lax.dot_general(split(x), y, dims, preferred_element_type=F32)
    return both[:rows] + both[rows:]


def dot_high(x, y, dims):
    return lax.dot_general(x, y, dims, precision=lax.Precision.HIGHEST, preferred_element_type=F32)


def inverse_factor(gram):
    size = gram.shape[0]
    row_at = lax.broadcasted_iota(jnp.int32, (size, size), 0)
    col_at = lax.broadcasted_iota(jnp.int32, (size, size), 1)
    eye = jnp.where(row_at == col_at, 1.0, 0.0).astype(F32)
    aug = jnp.concatenate([gram, eye], axis=1)
    width = 2 * size
    count = size // SUB
    blocks = [aug[SUB * i : SUB * (i + 1)] for i in range(count)]
    inner = lax.broadcasted_iota(jnp.int32, (SUB, width), 0)
    outs = []
    for b in range(count):
        cols = [
            [jnp.broadcast_to(blocks[i][:, SUB * b + k : SUB * b + k + 1], (SUB, width)) for i in range(b, count)]
            for k in range(SUB)
        ]
        top = blocks[b]
        scale = jnp.zeros((SUB, width), F32)
        rest = blocks[b + 1 :]
        for k in range(SUB):
            pivot = jnp.broadcast_to(cols[k][0][k : k + 1], (SUB, width))
            inv = 1.0 / pivot
            scale = jnp.where(inner == k, lax.rsqrt(pivot), scale)
            factors = [jnp.where(inner > k, cols[k][0], 0.0)] + cols[k][1:]
            for l in range(k + 1, SUB):
                mult = jnp.broadcast_to(cols[l][0][k : k + 1], (SUB, width)) * inv
                cols[l] = [c - f * mult for c, f in zip(cols[l], factors)]
            row = jnp.broadcast_to(top[k : k + 1], (SUB, width)) * inv
            top = top - factors[0] * row
            rest = [r - f * row for r, f in zip(rest, factors[1:])]
        outs.append((top * scale)[:, size:])
        blocks = blocks[: b + 1] + rest
    return jnp.concatenate(outs, axis=0)


def kernel(
    n_rep, n_shard, scale_factor,
    x_ref, c_ref, m_ref, q_ref,
    mom_out, right_out, up_out,
    left_part, left_in, left, ortho, right_part, right_in, right, sq_in, grad_part, grad_in, pad, turn,
    send, recv,
):
    rep, shard = lax.axis_index("rep"), lax.axis_index("shard")
    n_dev = n_rep * n_shard
    me = rep * n_shard + shard
    rank = q_ref.shape[1]
    out_total = c_ref.shape[1]
    rows, feats = m_ref.shape
    row_blocks = rank // SUB
    left_owners = row_blocks * (out_total // LANE)
    right_owners = row_blocks
    chunk = min(512, out_total)
    n_chunk = out_total // chunk
    per_tile = LANE // rows

    def device(index):
        return (index // n_shard, lax.rem(index, n_shard))

    def guarded(owners, total, index, fn):
        if owners == total:
            fn()
        else:
            pl.when(index < owners)(fn)

    def over(count, fn):
        if count == 1:
            fn(0)
        else:
            lax.fori_loop(0, count, lambda i, u: (fn(i), u)[1], 0)

    def lanes(i):
        if isinstance(i, int):
            return pl.ds(i * chunk, chunk)
        return pl.ds(pl.multiple_of(i * chunk, chunk), chunk)

    def copy(src, dst, k, target):
        return pltpu.make_async_remote_copy(
            src_ref=src, dst_ref=dst, send_sem=send.at[k], recv_sem=recv.at[k],
            device_id=target, device_id_type=MESH,
        )

    def drain(sem, ref):
        pltpu.make_async_copy(ref, ref, sem).wait()

    def tile(ref, t):
        r = pl.multiple_of(lax.rem(t, row_blocks) * SUB, SUB)
        c = pl.multiple_of((t // row_blocks) * LANE, LANE)
        return ref.at[pl.ds(r, SUB), pl.ds(c, LANE)]

    def band(b):
        return pl.ds(pl.multiple_of(b * SUB, SUB), SUB)

    barrier = pltpu.get_barrier_semaphore()

    def greet(p, u):
        pl.semaphore_signal(barrier, inc=1, device_id=device(lax.rem(me + p, n_dev)), device_id_type=MESH)
        return u

    lax.fori_loop(1, n_dev, greet, 0)

    x = x_ref[...]
    q_t = q_ref[...].T
    w_t = dot_split(q_t, x, NT)
    w_two = split(w_t)

    def left_chunk(i):
        both = lax.dot_general(w_two, c_ref[:, lanes(i)], NN, preferred_element_type=F32)
        left_part[:, lanes(i)] = both[:rank] + both[rank:]

    over(n_chunk, left_chunk)
    pad[...] = jnp.zeros_like(pad)
    half = lax.rem(rep, per_tile)
    my_rows = pl.ds(pl.multiple_of(half * rows, rows), rows)
    my_lanes = pl.ds(pl.multiple_of((rep // per_tile) * LANE, LANE), LANE)
    pad[my_rows, :] = m_ref[...]
    left_part[:, my_lanes] += dot_high(q_t, pad[...], NT)

    pl.semaphore_wait(barrier, n_dev - 1)

    def send_left(p, u):
        t = lax.rem(me + p, n_dev)
        guarded(left_owners, n_dev, t, lambda: copy(tile(left_part, t), left_in.at[me], 0, device(t)).start())
        return u

    lax.fori_loop(1, n_dev, send_left, 0)

    def grad_chunk(i):
        g = lax.dot_general(c_ref[:, lanes(i)], x, TN, preferred_element_type=F32)
        grad_part[lanes(i), :] = g

    over(n_chunk, grad_chunk)

    def own_left():
        left_in[me] = tile(left_part, me)[...]
        drain(recv.at[0], left_in.at[pl.ds(0, n_dev - 1)])
        tile(left, me)[...] = jnp.sum(left_in[...], axis=0)

        def give(p, u):
            copy(tile(left, me), tile(left, me), 1, device(lax.rem(me + p, n_dev))).start()
            return u

        lax.fori_loop(1, n_dev, give, 0)

    guarded(left_owners, n_dev, me, own_left)

    def grad_rows(r):
        return pl.ds(pl.multiple_of(r * rows, rows), rows)

    def send_grad(p, u):
        t = lax.rem(rep + p, n_rep)
        copy(grad_part.at[grad_rows(t), :], grad_in.at[rep], 2, (t, shard)).start()
        return u

    if left_owners == n_dev:
        drain(recv.at[1], left_in.at[pl.ds(0, n_dev - 1)])
        lax.fori_loop(1, n_rep, send_grad, 0)
    else:
        lax.fori_loop(1, n_rep, send_grad, 0)

        @pl.when(me < left_owners)
        def _():
            drain(recv.at[1], left_in.at[pl.ds(0, left_owners - 1)])

        @pl.when(me >= left_owners)
        def _():
            drain(recv.at[1], left_in.at[pl.ds(0, left_owners)])

    grad_in[rep] = grad_part[grad_rows(rep), :]

    if n_chunk == 1:
        whole = left[...]
        gram = dot_high(whole, whole, NT)
    else:
        gram = lax.fori_loop(
            0, n_chunk,
            lambda i, g: g + dot_high(left[:, lanes(i)], left[:, lanes(i)], NT),
            jnp.zeros((rank, rank), F32),
        )
    inv = inverse_factor(gram)

    def ortho_chunk(i):
        ortho[:, lanes(i)] = dot_high(inv, left[:, lanes(i)], NN)

    over(n_chunk, ortho_chunk)
    if n_chunk == 1:
        v_t = dot_split(ortho[...], c_ref[...], NT)
    else:
        v_t = lax.fori_loop(
            0, n_chunk,
            lambda i, v: v + dot_split(ortho[:, lanes(i)], c_ref[:, lanes(i)], NT),
            jnp.zeros((rank, c_ref.shape[0]), F32),
        )
    mine_t = ortho[:, my_lanes]
    right_part[...] = dot_split(v_t, x, NN) + dot_high(
        mine_t, pad[...], NN
    )

    def send_right(p, u):
        t = lax.rem(rep + p, n_rep)
        guarded(
            right_owners, n_rep, t,
            lambda: copy(right_part.at[band(t), :], right_in.at[rep], 3, (t, shard)).start(),
        )
        return u

    lax.fori_loop(1, n_rep, send_right, 0)
    pad_turn = mine_t.T

    def own_right():
        right_in[rep] = right_part[band(rep), :]
        drain(recv.at[3], right_in.at[pl.ds(0, n_rep - 1)])
        total = jnp.sum(right_in[...], axis=0)
        right[band(rep), :] = total
        sq_in[shard, band(rep), :] = jnp.broadcast_to(jnp.sum(total * total, axis=1, keepdims=True), (SUB, LANE))

        def give_right(p, u):
            copy(right.at[band(rep), :], right.at[band(rep), :], 4, (lax.rem(rep + p, n_rep), shard)).start()
            return u

        lax.fori_loop(1, n_rep, give_right, 0)

        def give_sq(p, u):
            place = sq_in.at[shard, band(rep), :]
            copy(place, place, 5, device(lax.rem(me + p, n_dev))).start()
            return u

        lax.fori_loop(1, n_dev, give_sq, 0)

    guarded(right_owners, n_rep, rep, own_right)

    drain(recv.at[2], grad_in.at[pl.ds(0, n_rep - 1)])
    blended = m_ref[...] + lax.fori_loop(1, n_rep, lambda r, g: g + grad_in[r], grad_in[0])
    turn[...] = pad_turn
    mine = turn[my_rows, :]

    def finish_recv(n_right, n_sq):
        drain(recv.at[4], right_in.at[pl.ds(0, n_right)])
        flat = left_in.at[pl.ds(0, n_sq)]
        drain(recv.at[5], flat)

    sq_all = right_owners * n_shard
    if right_owners == n_rep:
        finish_recv(right_owners - 1, sq_all - 1)
    else:
        @pl.when(rep < right_owners)
        def _():
            finish_recv(right_owners - 1, sq_all - 1)

        @pl.when(rep >= right_owners)
        def _():
            finish_recv(right_owners, sq_all)

    right_t = right[...]
    mom_out[...] = blended - 0.05 * dot_high(mine, right_t, NN)
    norm = jnp.sqrt(jnp.sum(sq_in[...], axis=0) + 1e-06)
    factor_t = jnp.concatenate(
        [right_t[:, LANE * i : LANE * (i + 1)] / norm for i in range(feats // LANE)], axis=1
    )
    up_out[...] = (scale_factor * dot_high(mine, factor_t, NN)).astype(up_out.dtype)
    right_out[...] = factor_t.T

    def left_sent(n):
        drain(send.at[0], left_in.at[pl.ds(0, n)])

    if left_owners == n_dev:
        left_sent(n_dev - 1)
        drain(send.at[1], left_in.at[pl.ds(0, n_dev - 1)])
    else:
        @pl.when(me < left_owners)
        def _():
            left_sent(left_owners - 1)
            drain(send.at[1], left_in.at[pl.ds(0, n_dev - 1)])

        @pl.when(me >= left_owners)
        def _():
            left_sent(left_owners)

    drain(send.at[2], grad_in.at[pl.ds(0, n_rep - 1)])

    def right_sent():
        drain(send.at[4], right_in.at[pl.ds(0, n_rep - 1)])
        drain(send.at[5], left_in.at[pl.ds(0, n_dev - 1)])

    if right_owners == n_rep:
        drain(send.at[3], right_in.at[pl.ds(0, n_rep - 1)])
        right_sent()
    else:
        @pl.when(rep < right_owners)
        def _():
            drain(send.at[3], right_in.at[pl.ds(0, right_owners - 1)])
            right_sent()

        @pl.when(rep >= right_owners)
        def _():
            drain(send.at[3], right_in.at[pl.ds(0, right_owners)])


def body(n_rep, n_shard, inputs, cotangent, momentum, right_prev):
    out_total = cotangent.shape[1]
    rows, feats = momentum.shape
    rank = right_prev.shape[1]
    n_dev = n_rep * n_shard
    scale_factor = (out_total * feats * n_shard / rank) ** 0.5
    vmem = pl.BlockSpec(memory_space=pltpu.VMEM)
    return pl.pallas_call(
        functools.partial(kernel, n_rep, n_shard, scale_factor),
        out_shape=(
            jax.ShapeDtypeStruct((rows, feats), F32),
            jax.ShapeDtypeStruct((feats, rank), F32),
            jax.ShapeDtypeStruct((rows, feats), BF16),
        ),
        in_specs=[vmem] * 4,
        out_specs=(vmem,) * 3,
        scratch_shapes=[
            pltpu.VMEM((rank, out_total), F32),
            pltpu.VMEM((n_dev, SUB, LANE), F32),
            pltpu.VMEM((rank, out_total), F32),
            pltpu.VMEM((rank, out_total), F32),
            pltpu.VMEM((rank, feats), F32),
            pltpu.VMEM((n_rep, SUB, feats), F32),
            pltpu.VMEM((rank, feats), F32),
            pltpu.VMEM((n_shard, rank, LANE), F32),
            pltpu.VMEM((out_total, feats), F32),
            pltpu.VMEM((n_rep, rows, feats), F32),
            pltpu.VMEM((LANE, feats), F32),
            pltpu.VMEM((LANE, rank), F32),
            pltpu.SemaphoreType.DMA((6,)),
            pltpu.SemaphoreType.DMA((6,)),
        ],
        compiler_params=pltpu.CompilerParams(
            collective_id=0, has_side_effects=True, vmem_limit_bytes=48 * 1024 * 1024
        ),
    )(inputs, cotangent, momentum, right_prev)


def solution(mesh):
    return jax.shard_map(
        functools.partial(body, mesh.shape["rep"], mesh.shape["shard"]),
        mesh=mesh,
        in_specs=(P("rep", "shard"), P("rep", None), P("rep", "shard"), P("shard", None)),
        out_specs=(P("rep", "shard"), P("shard", None), P("rep", "shard")),
        check_vma=False,
    )
```

```python
import functools

import jax
import jax.numpy as jnp
from jax import lax
from jax.experimental import pallas as pl
from jax.experimental.pallas import tpu as pltpu
from jax.sharding import PartitionSpec as P

MESH = pl.DeviceIdType.MESH
F32, BF16 = jnp.float32, jnp.bfloat16
SUB, LANE = 8, 128
SLICES, CUTS = 8, (2, 6)
NT = (((1,), (1,)), ((), ()))
NN = (((1,), (0,)), ((), ()))
TN = (((0,), (0,)), ((), ()))


def split(x):
    hi = x.astype(BF16)
    rest = x - hi.astype(F32)
    mid = rest.astype(BF16)
    low = (rest - mid.astype(F32)).astype(BF16)
    return jnp.concatenate([hi, mid, low], axis=0)


def fold(both):
    rows = both.shape[0] // 3
    return both[:rows] + (both[rows : 2 * rows] + both[2 * rows :])


def dot_split(x, y, dims):
    return fold(lax.dot_general(split(x), y, dims, preferred_element_type=F32))


def dot_high(x, y, dims):
    return lax.dot_general(x, y, dims, precision=lax.Precision.HIGHEST, preferred_element_type=F32)


def inverse_factor(gram):
    size = gram.shape[0]
    row_at = lax.broadcasted_iota(jnp.int32, (size, size), 0)
    col_at = lax.broadcasted_iota(jnp.int32, (size, size), 1)
    eye = jnp.where(row_at == col_at, 1.0, 0.0).astype(F32)
    aug = jnp.concatenate([gram, eye], axis=1)
    width = 2 * size
    count = size // SUB
    blocks = [aug[SUB * i : SUB * (i + 1)] for i in range(count)]
    inner = lax.broadcasted_iota(jnp.int32, (SUB, width), 0)
    outs = []
    for b in range(count):
        cols = [
            [jnp.broadcast_to(blocks[i][:, SUB * b + k : SUB * b + k + 1], (SUB, width)) for i in range(b, count)]
            for k in range(SUB)
        ]
        top = blocks[b]
        scale = jnp.zeros((SUB, width), F32)
        rest = blocks[b + 1 :]
        for k in range(SUB):
            pivot = jnp.broadcast_to(cols[k][0][k : k + 1], (SUB, width))
            inv = 1.0 / pivot
            scale = jnp.where(inner == k, lax.rsqrt(pivot), scale)
            factors = [jnp.where(inner > k, cols[k][0], 0.0)] + cols[k][1:]
            for l in range(k + 1, SUB):
                mult = jnp.broadcast_to(cols[l][0][k : k + 1], (SUB, width)) * inv
                cols[l] = [c - f * mult for c, f in zip(cols[l], factors)]
            row = jnp.broadcast_to(top[k : k + 1], (SUB, width)) * inv
            top = top - factors[0] * row
            rest = [r - f * row for r, f in zip(rest, factors[1:])]
        outs.append((top * scale)[:, size:])
        blocks = blocks[: b + 1] + rest
    return jnp.concatenate(outs, axis=0)


def kernel(
    n_rep, n_shard, scale_factor,
    x_hbm, c_hbm, m_hbm, q_hbm,
    out_ref,
    left_part, left_in, left, right_part, right_in, right, sq_in, grad_part, grad_in, pad, turn,
    x_ref, c_ref, m_ref, q_ref, send, recv, load,
):
    rep, shard = lax.axis_index("rep"), lax.axis_index("shard")
    n_dev = n_rep * n_shard
    me = rep * n_shard + shard
    rank = q_ref.shape[0]
    out_total = c_ref.shape[1]
    rows, feats = m_ref.shape
    row_blocks = rank // SUB
    left_owners = row_blocks * (out_total // LANE)
    share = max(SUB, LANE // n_rep)
    right_owners = LANE // share
    chunk = min(512, out_total)
    n_chunk = out_total // chunk
    per_tile = LANE // rows

    def device(index):
        return (index // n_shard, lax.rem(index, n_shard))

    def guarded(owners, total, index, fn):
        if owners == total:
            fn()
        else:
            pl.when(index < owners)(fn)

    def over(count, fn):
        if count == 1:
            fn(0)
        else:
            lax.fori_loop(0, count, lambda i, u: (fn(i), u)[1], 0)

    def lanes(i):
        if isinstance(i, int):
            return pl.ds(i * chunk, chunk)
        return pl.ds(pl.multiple_of(i * chunk, chunk), chunk)

    def copy(src, dst, k, target):
        return pltpu.make_async_remote_copy(
            src_ref=src, dst_ref=dst, send_sem=send.at[k], recv_sem=recv.at[k],
            device_id=target, device_id_type=MESH,
        )

    def drain(sem, ref):
        pltpu.make_async_copy(ref, ref, sem).wait()

    def tile(ref, t):
        r = pl.multiple_of(lax.rem(t, row_blocks) * SUB, SUB)
        c = pl.multiple_of((t // row_blocks) * LANE, LANE)
        return ref.at[pl.ds(r, SUB), pl.ds(c, LANE)]

    def band(b):
        return pl.ds(pl.multiple_of(b * share, SUB), share)

    loads = [
        pltpu.make_async_copy(src, dst, load.at[i])
        for i, (src, dst) in enumerate(((q_hbm, q_ref), (x_hbm, x_ref), (m_hbm, m_ref), (c_hbm, c_ref)))
    ]
    for each in loads:
        each.start()

    barrier = pltpu.get_barrier_semaphore()

    def greet(p, u):
        pl.semaphore_signal(barrier, inc=1, device_id=device(lax.rem(me + p, n_dev)), device_id_type=MESH)
        return u

    lax.fori_loop(1, n_dev, greet, 0)

    loads[0].wait()
    loads[1].wait()
    x = x_ref[...]
    q_t = q_ref[...]
    w_t = dot_split(q_t, x, NT)
    w_terms = split(w_t)
    loads[2].wait()
    loads[3].wait()

    def left_chunk(i):
        both = lax.dot_general(w_terms, c_ref[:, lanes(i)], NN, preferred_element_type=F32)
        left_part[:, lanes(i)] = fold(both)

    over(n_chunk, left_chunk)
    pad[...] = jnp.zeros_like(pad)
    half = lax.rem(rep, per_tile)
    my_rows = pl.ds(pl.multiple_of(half * rows, rows), rows)
    my_lanes = pl.ds(pl.multiple_of((rep // per_tile) * LANE, LANE), LANE)
    pad[my_rows, :] = m_ref[...]
    left_part[:, my_lanes] += dot_high(q_t, pad[...], NT)

    pl.semaphore_wait(barrier, n_dev - 1)

    def send_left(p, u):
        t = lax.rem(me + p, n_dev)
        guarded(left_owners, n_dev, t, lambda: copy(tile(left_part, t), left_in.at[me], 0, device(t)).start())
        return u

    lax.fori_loop(1, n_dev, send_left, 0)

    step = rows // SLICES

    def grad_rows(r):
        return pl.ds(pl.multiple_of(r * rows, rows), rows)

    def send_grad(first, last):
        if first == last:
            return

        def one(p, u):
            t = lax.rem(rep + p, n_rep)
            n = (last - first) * step
            src = pl.ds(pl.multiple_of(t * rows + first * step, SUB), n)
            copy(grad_part.at[src, :], grad_in.at[rep, pl.ds(first * step, n), :], 2, (t, shard)).start()
            return u

        lax.fori_loop(1, n_rep, one, 0)

    def grad_chunk(i):
        g = lax.dot_general(c_ref[:, lanes(i)], x, TN, preferred_element_type=F32)
        grad_part[lanes(i), :] = g

    over(n_chunk, grad_chunk)
    send_grad(0, CUTS[0])

    def own_left():
        left_in[me] = tile(left_part, me)[...]
        drain(recv.at[0], left_in.at[pl.ds(0, n_dev - 1)])
        tile(left, me)[...] = jnp.sum(left_in[...], axis=0)

        def give(p, u):
            copy(tile(left, me), tile(left, me), 1, device(lax.rem(me + p, n_dev))).start()
            return u

        lax.fori_loop(1, n_dev, give, 0)

    guarded(left_owners, n_dev, me, own_left)

    send_grad(CUTS[0], CUTS[1])
    if left_owners == n_dev:
        drain(recv.at[1], left_in.at[pl.ds(0, n_dev - 1)])
    else:
        @pl.when(me < left_owners)
        def _():
            drain(recv.at[1], left_in.at[pl.ds(0, left_owners - 1)])

        @pl.when(me >= left_owners)
        def _():
            drain(recv.at[1], left_in.at[pl.ds(0, left_owners)])

    grad_in[rep] = grad_part[grad_rows(rep), :]

    if n_chunk == 1:
        v_t = dot_split(left[...], c_ref[...], NT)
    else:
        v_t = lax.fori_loop(
            0, n_chunk,
            lambda i, v: v + dot_split(left[:, lanes(i)], c_ref[:, lanes(i)], NT),
            jnp.zeros((rank, c_ref.shape[0]), F32),
        )
    mine_t = left[:, my_lanes]
    cross_t = dot_split(v_t, x, NN) + dot_high(mine_t, pad[...], NN)
    right_part[...] = jnp.concatenate([cross_t[:, :LANE], cross_t[:, LANE:]], axis=0).T

    def send_right(p, u):
        t = lax.rem(rep + p, n_rep)
        guarded(
            right_owners, n_rep, t,
            lambda: copy(right_part.at[band(t), :], right_in.at[rep], 3, (t, shard)).start(),
        )
        return u

    lax.fori_loop(1, n_rep, send_right, 0)
    send_grad(CUTS[1], SLICES)

    if n_chunk == 1:
        whole = left[...]
        gram = dot_high(whole, whole, NT)
    else:
        gram = lax.fori_loop(
            0, n_chunk,
            lambda i, g: g + dot_high(left[:, lanes(i)], left[:, lanes(i)], NT),
            jnp.zeros((rank, rank), F32),
        )
    inv = inverse_factor(gram)
    turn[...] = mine_t.T
    mine = dot_high(turn[my_rows, :], inv, NT)
    none = jnp.zeros((rank, rank), F32)
    inv_two = jnp.concatenate(
        [jnp.concatenate([inv, none], axis=1), jnp.concatenate([none, inv], axis=1)], axis=0
    )

    def own_right():
        right_in[rep] = right_part[band(rep), :]
        drain(recv.at[3], right_in.at[pl.ds(0, n_rep - 1)])
        total = dot_high(jnp.sum(right_in[...], axis=0), inv_two, NT)
        right[band(rep), :] = total
        sq_in[me] = jnp.broadcast_to(jnp.sum(total * total, axis=0, keepdims=True), (SUB, LANE))

        def give_right(p, u):
            copy(right.at[band(rep), :], right.at[band(rep), :], 4, (lax.rem(rep + p, n_rep), shard)).start()
            return u

        lax.fori_loop(1, n_rep, give_right, 0)

        def give_sq(p, u):
            copy(sq_in.at[me], sq_in.at[me], 5, device(lax.rem(me + p, n_dev))).start()
            return u

        lax.fori_loop(1, n_dev, give_sq, 0)

    guarded(right_owners, n_rep, rep, own_right)

    drain(recv.at[2], grad_in.at[pl.ds(0, n_rep - 1)])
    blended = m_ref[...] + lax.fori_loop(1, n_rep, lambda r, g: g + grad_in[r], grad_in[0])

    def finish_recv(n_right, n_sq):
        drain(recv.at[4], right_in.at[pl.ds(0, n_right)])
        flat = left_in.at[pl.ds(0, n_sq)]
        drain(recv.at[5], flat)

    sq_all = right_owners * n_shard
    if right_owners == n_rep:
        finish_recv(right_owners - 1, sq_all - 1)
    else:
        @pl.when(rep < right_owners)
        def _():
            finish_recv(right_owners - 1, sq_all - 1)

        @pl.when(rep >= right_owners)
        def _():
            finish_recv(right_owners, sq_all)

    def wide(packed):
        t = packed.T
        return jnp.concatenate([t[:rank], t[rank:]], axis=1)

    packed = right[...]
    right_t = wide(packed)
    out_ref[0] = blended - 0.05 * dot_high(mine, right_t, NN)
    halves = jnp.sum(jnp.sum(sq_in[pl.ds(0, sq_all)], axis=0), axis=0, keepdims=True) * (1.0 / SUB)
    column_sq = halves[:, :rank] + halves[:, rank:]
    norm = jnp.sqrt(column_sq + 1e-06)
    factor_t = wide(packed / jnp.concatenate([norm, norm], axis=1))
    out_ref[2] = scale_factor * dot_high(mine, factor_t, NN)
    out_ref[1] = factor_t

    def left_sent(n):
        drain(send.at[0], left_in.at[pl.ds(0, n)])

    if left_owners == n_dev:
        left_sent(n_dev - 1)
        drain(send.at[1], left_in.at[pl.ds(0, n_dev - 1)])
    else:
        @pl.when(me < left_owners)
        def _():
            left_sent(left_owners - 1)
            drain(send.at[1], left_in.at[pl.ds(0, n_dev - 1)])

        @pl.when(me >= left_owners)
        def _():
            left_sent(left_owners)

    drain(send.at[2], grad_in.at[pl.ds(0, n_rep - 1)])

    def right_sent():
        drain(send.at[4], right_in.at[pl.ds(0, n_rep - 1)])
        drain(send.at[5], left_in.at[pl.ds(0, n_dev - 1)])

    if right_owners == n_rep:
        drain(send.at[3], right_in.at[pl.ds(0, n_rep - 1)])
        right_sent()
    else:
        @pl.when(rep < right_owners)
        def _():
            drain(send.at[3], right_in.at[pl.ds(0, right_owners - 1)])
            right_sent()

        @pl.when(rep >= right_owners)
        def _():
            drain(send.at[3], right_in.at[pl.ds(0, right_owners)])


def body(n_rep, n_shard, inputs, cotangent, momentum, right_prev):
    out_total = cotangent.shape[1]
    rows, feats = momentum.shape
    rank = right_prev.shape[1]
    n_dev = n_rep * n_shard
    scale_factor = (out_total * feats * n_shard / rank) ** 0.5
    share = max(SUB, LANE // n_rep)
    assert 2 * rank == LANE and feats == 2 * LANE
    vmem = pl.BlockSpec(memory_space=pltpu.VMEM)
    results = pl.pallas_call(
        functools.partial(kernel, n_rep, n_shard, scale_factor),
        out_shape=jax.ShapeDtypeStruct((3, rows, feats), F32),
        in_specs=[pl.BlockSpec(memory_space=pltpu.HBM)] * 4,
        out_specs=vmem,
        scratch_shapes=[
            pltpu.VMEM((rank, out_total), F32),
            pltpu.VMEM((n_dev, SUB, LANE), F32),
            pltpu.VMEM((rank, out_total), F32),
            pltpu.VMEM((LANE, LANE), F32),
            pltpu.VMEM((n_rep, share, LANE), F32),
            pltpu.VMEM((LANE, LANE), F32),
            pltpu.VMEM((n_dev, SUB, LANE), F32),
            pltpu.VMEM((out_total, feats), F32),
            pltpu.VMEM((n_rep, rows, feats), F32),
            pltpu.VMEM((LANE, feats), F32),
            pltpu.VMEM((LANE, rank), F32),
            pltpu.VMEM(inputs.shape, BF16),
            pltpu.VMEM(cotangent.shape, BF16),
            pltpu.VMEM(momentum.shape, F32),
            pltpu.VMEM((rank, feats), F32),
            pltpu.SemaphoreType.DMA((6,)),
            pltpu.SemaphoreType.DMA((6,)),
            pltpu.SemaphoreType.DMA((4,)),
        ],
        compiler_params=pltpu.CompilerParams(
            collective_id=0, has_side_effects=True, vmem_limit_bytes=67043328
        ),
    )(inputs, cotangent, momentum, right_prev.T)
    return results[0], results[1].T, results[2].astype(BF16)


def solution(mesh):
    return jax.shard_map(
        functools.partial(body, mesh.shape["rep"], mesh.shape["shard"]),
        mesh=mesh,
        in_specs=(P("rep", "shard"), P("rep", None), P("rep", "shard"), P("shard", None)),
        out_specs=(P("rep", "shard"), P("shard", None), P("rep", "shard")),
        check_vma=False,
    )
```

```python
import functools

import jax
import jax.numpy as jnp
from jax import lax
from jax.experimental import pallas as pl
from jax.experimental.pallas import tpu as pltpu
from jax.sharding import PartitionSpec as P

MESH = pl.DeviceIdType.MESH
F32, BF16 = jnp.float32, jnp.bfloat16
SUB, LANE = 8, 128
UNIT, PAIR_CUT, LINE_CUTS = 8, 4, (0, 8)
NT = (((1,), (1,)), ((), ()))
NN = (((1,), (0,)), ((), ()))
TN = (((0,), (0,)), ((), ()))


def split(x):
    hi = x.astype(BF16)
    rest = x - hi.astype(F32)
    mid = rest.astype(BF16)
    low = (rest - mid.astype(F32)).astype(BF16)
    return jnp.concatenate([hi, mid, low], axis=0)


def fold(both):
    rows = both.shape[0] // 3
    return both[:rows] + (both[rows : 2 * rows] + both[2 * rows :])


def dot_split(x, y, dims):
    return fold(lax.dot_general(split(x), y, dims, preferred_element_type=F32))


def dot_high(x, y, dims):
    return lax.dot_general(x, y, dims, precision=lax.Precision.HIGHEST, preferred_element_type=F32)


def inverse_factor(gram):
    size = gram.shape[0]
    row_at = lax.broadcasted_iota(jnp.int32, (size, size), 0)
    col_at = lax.broadcasted_iota(jnp.int32, (size, size), 1)
    eye = jnp.where(row_at == col_at, 1.0, 0.0).astype(F32)
    aug = jnp.concatenate([gram, eye], axis=1)
    width = 2 * size
    count = size // SUB
    blocks = [aug[SUB * i : SUB * (i + 1)] for i in range(count)]
    inner = lax.broadcasted_iota(jnp.int32, (SUB, width), 0)
    outs = []
    for b in range(count):
        cols = [
            [jnp.broadcast_to(blocks[i][:, SUB * b + k : SUB * b + k + 1], (SUB, width)) for i in range(b, count)]
            for k in range(SUB)
        ]
        top = blocks[b]
        scale = jnp.zeros((SUB, width), F32)
        rest = blocks[b + 1 :]
        for k in range(SUB):
            pivot = jnp.broadcast_to(cols[k][0][k : k + 1], (SUB, width))
            inv = 1.0 / pivot
            scale = jnp.where(inner == k, lax.rsqrt(pivot), scale)
            factors = [jnp.where(inner > k, cols[k][0], 0.0)] + cols[k][1:]
            for l in range(k + 1, SUB):
                mult = jnp.broadcast_to(cols[l][0][k : k + 1], (SUB, width)) * inv
                cols[l] = [c - f * mult for c, f in zip(cols[l], factors)]
            row = jnp.broadcast_to(top[k : k + 1], (SUB, width)) * inv
            top = top - factors[0] * row
            rest = [r - f * row for r, f in zip(rest, factors[1:])]
        outs.append((top * scale)[:, size:])
        blocks = blocks[: b + 1] + rest
    return jnp.concatenate(outs, axis=0)


def kernel(
    n_rep, n_shard, scale_factor,
    x_hbm, c_hbm, m_hbm, q_hbm,
    out_ref,
    left_part, left_in, left, right_part, right_in, right, sq_in, grad_part, grad_in, pair_in, pair_sum, pad, turn,
    x_ref, c_ref, m_ref, q_ref, send, recv, load,
):
    rep, shard = lax.axis_index("rep"), lax.axis_index("shard")
    n_dev = n_rep * n_shard
    me = rep * n_shard + shard
    rank = q_ref.shape[0]
    out_total = c_ref.shape[1]
    rows, feats = m_ref.shape
    row_blocks = rank // SUB
    left_owners = row_blocks * (out_total // LANE)
    share = max(SUB, LANE // n_rep)
    right_owners = LANE // share
    chunk = min(512, out_total)
    n_chunk = out_total // chunk
    per_tile = LANE // rows

    def device(index):
        return (index // n_shard, lax.rem(index, n_shard))

    def guarded(owners, total, index, fn):
        if owners == total:
            fn()
        else:
            pl.when(index < owners)(fn)

    def over(count, fn):
        if count == 1:
            fn(0)
        else:
            lax.fori_loop(0, count, lambda i, u: (fn(i), u)[1], 0)

    def lanes(i):
        if isinstance(i, int):
            return pl.ds(i * chunk, chunk)
        return pl.ds(pl.multiple_of(i * chunk, chunk), chunk)

    def copy(src, dst, k, target):
        return pltpu.make_async_remote_copy(
            src_ref=src, dst_ref=dst, send_sem=send.at[k], recv_sem=recv.at[k],
            device_id=target, device_id_type=MESH,
        )

    def drain(sem, ref):
        pltpu.make_async_copy(ref, ref, sem).wait()

    def tile(ref, t):
        r = pl.multiple_of(lax.rem(t, row_blocks) * SUB, SUB)
        c = pl.multiple_of((t // row_blocks) * LANE, LANE)
        return ref.at[pl.ds(r, SUB), pl.ds(c, LANE)]

    def band(b):
        return pl.ds(pl.multiple_of(b * share, SUB), share)

    loads = [
        pltpu.make_async_copy(src, dst, load.at[i])
        for i, (src, dst) in enumerate(((q_hbm, q_ref), (x_hbm, x_ref), (m_hbm, m_ref), (c_hbm, c_ref)))
    ]
    for each in loads:
        each.start()

    barrier = pltpu.get_barrier_semaphore()

    def greet(p, u):
        pl.semaphore_signal(barrier, inc=1, device_id=device(lax.rem(me + p, n_dev)), device_id_type=MESH)
        return u

    lax.fori_loop(1, n_dev, greet, 0)

    loads[0].wait()
    loads[1].wait()
    x = x_ref[...]
    q_t = q_ref[...]
    w_t = dot_split(q_t, x, NT)
    w_terms = split(w_t)
    loads[2].wait()
    loads[3].wait()

    def left_chunk(i):
        both = lax.dot_general(w_terms, c_ref[:, lanes(i)], NN, preferred_element_type=F32)
        left_part[:, lanes(i)] = fold(both)

    over(n_chunk, left_chunk)
    pad[...] = jnp.zeros_like(pad)
    half = lax.rem(rep, per_tile)
    my_rows = pl.ds(pl.multiple_of(half * rows, rows), rows)
    my_lanes = pl.ds(pl.multiple_of((rep // per_tile) * LANE, LANE), LANE)
    pad[my_rows, :] = m_ref[...]
    left_part[:, my_lanes] += dot_high(q_t, pad[...], NT)

    pl.semaphore_wait(barrier, n_dev - 1)

    def send_left(p, u):
        t = lax.rem(me + p, n_dev)
        guarded(left_owners, n_dev, t, lambda: copy(tile(left_part, t), left_in.at[me], 0, device(t)).start())
        return u

    lax.fori_loop(1, n_dev, send_left, 0)

    n_line = n_rep // 2
    line, side = rep // 2, lax.rem(rep, 2)
    unit = rows // UNIT

    def span(first, last):
        return pl.ds(first * unit, (last - first) * unit)

    def send_pair(first, last, k):
        if first == last:
            return
        part = span(first, last)
        copy(
            grad_part.at[1 - side, :, part, :], pair_in.at[:, part, :], k, (2 * line + 1 - side, shard)
        ).start()

    def take_pair(first, last, k):
        if first == last:
            return
        part = span(first, last)
        drain(recv.at[k], pair_in.at[:, part, :])
        for h in range(n_line) if n_line <= 8 else ():
            pair_sum[h, part, :] = grad_part[side, h, part, :] + pair_in[h, part, :]
        if n_line > 8:
            def add(h, u):
                pair_sum[h, part, :] = grad_part[side, h, part, :] + pair_in[h, part, :]
                return u

            lax.fori_loop(0, n_line, add, 0)

    def send_line(first, last):
        if first == last:
            return
        part = span(first, last)

        def one(p, u):
            t = lax.rem(line + p, n_line)
            copy(pair_sum.at[t, part, :], grad_in.at[line, part, :], 2, (2 * t + side, shard)).start()
            return u

        lax.fori_loop(1, n_line, one, 0)

    def grad_chunk(i):
        g = lax.dot_general(c_ref[:, lanes(i)], x, TN, preferred_element_type=F32)
        for r in range(chunk // rows):
            at = i * (chunk // rows) + r
            grad_part[at % 2, at // 2] = g[r * rows : (r + 1) * rows]

    over(n_chunk, grad_chunk)
    send_pair(0, PAIR_CUT, 6)

    def own_left():
        left_in[me] = tile(left_part, me)[...]
        drain(recv.at[0], left_in.at[pl.ds(0, n_dev - 1)])
        tile(left, me)[...] = jnp.sum(left_in[...], axis=0)

        def give(p, u):
            copy(tile(left, me), tile(left, me), 1, device(lax.rem(me + p, n_dev))).start()
            return u

        lax.fori_loop(1, n_dev, give, 0)

    guarded(left_owners, n_dev, me, own_left)

    send_pair(PAIR_CUT, UNIT, 7)
    if left_owners == n_dev:
        drain(recv.at[1], left_in.at[pl.ds(0, n_dev - 1)])
    else:
        @pl.when(me < left_owners)
        def _():
            drain(recv.at[1], left_in.at[pl.ds(0, left_owners - 1)])

        @pl.when(me >= left_owners)
        def _():
            drain(recv.at[1], left_in.at[pl.ds(0, left_owners)])


    take_pair(0, PAIR_CUT, 6)
    send_line(0, LINE_CUTS[0])

    if n_chunk == 1:
        v_t = dot_split(left[...], c_ref[...], NT)
    else:
        v_t = lax.fori_loop(
            0, n_chunk,
            lambda i, v: v + dot_split(left[:, lanes(i)], c_ref[:, lanes(i)], NT),
            jnp.zeros((rank, c_ref.shape[0]), F32),
        )
    mine_t = left[:, my_lanes]
    cross_t = dot_split(v_t, x, NN) + dot_high(mine_t, pad[...], NN)
    right_part[...] = jnp.concatenate([cross_t[:, :LANE], cross_t[:, LANE:]], axis=0).T

    def send_right(p, u):
        t = lax.rem(rep + p, n_rep)
        guarded(
            right_owners, n_rep, t,
            lambda: copy(right_part.at[band(t), :], right_in.at[rep], 3, (t, shard)).start(),
        )
        return u

    lax.fori_loop(1, n_rep, send_right, 0)
    take_pair(PAIR_CUT, UNIT, 7)
    send_line(LINE_CUTS[0], LINE_CUTS[1])

    if n_chunk == 1:
        whole = left[...]
        gram = dot_high(whole, whole, NT)
    else:
        gram = lax.fori_loop(
            0, n_chunk,
            lambda i, g: g + dot_high(left[:, lanes(i)], left[:, lanes(i)], NT),
            jnp.zeros((rank, rank), F32),
        )
    inv = inverse_factor(gram)
    turn[...] = mine_t.T
    mine = dot_high(turn[my_rows, :], inv, NT)
    none = jnp.zeros((rank, rank), F32)
    inv_two = jnp.concatenate(
        [jnp.concatenate([inv, none], axis=1), jnp.concatenate([none, inv], axis=1)], axis=0
    )

    def own_right():
        right_in[rep] = right_part[band(rep), :]
        drain(recv.at[3], right_in.at[pl.ds(0, n_rep - 1)])
        total = dot_high(jnp.sum(right_in[...], axis=0), inv_two, NT)
        right[band(rep), :] = total
        sq_in[me] = jnp.sum(total * total, axis=0, keepdims=True)

        def give_right(p, u):
            copy(right.at[band(rep), :], right.at[band(rep), :], 4, (lax.rem(rep + p, n_rep), shard)).start()
            return u

        lax.fori_loop(1, n_rep, give_right, 0)

        def give_sq(p, u):
            copy(sq_in.at[me], sq_in.at[me], 5, device(lax.rem(me + p, n_dev))).start()
            return u

        lax.fori_loop(1, n_dev, give_sq, 0)

    guarded(right_owners, n_rep, rep, own_right)

    send_line(LINE_CUTS[1], UNIT)

    grad_in[line] = pair_sum[line]
    drain(recv.at[2], grad_in.at[pl.ds(0, n_line - 1)])
    blended = m_ref[...] + lax.fori_loop(1, n_line, lambda r, g: g + grad_in[r], grad_in[0])

    def finish_recv(n_right, n_sq):
        drain(recv.at[4], right_in.at[pl.ds(0, n_right)])
        flat = sq_in.at[pl.ds(0, n_sq)]
        drain(recv.at[5], flat)

    sq_all = right_owners * n_shard
    if right_owners == n_rep:
        finish_recv(right_owners - 1, sq_all - 1)
    else:
        @pl.when(rep < right_owners)
        def _():
            finish_recv(right_owners - 1, sq_all - 1)

        @pl.when(rep >= right_owners)
        def _():
            finish_recv(right_owners, sq_all)

    def wide(packed):
        t = packed.T
        return jnp.concatenate([t[:rank], t[rank:]], axis=1)

    packed = right[...]
    right_t = wide(packed)
    out_ref[0] = blended - 0.05 * dot_high(mine, right_t, NN)
    halves = jnp.sum(sq_in[pl.ds(0, sq_all)], axis=0)
    column_sq = halves[:, :rank] + halves[:, rank:]
    norm = jnp.sqrt(column_sq + 1e-06)
    factor_t = wide(packed / jnp.concatenate([norm, norm], axis=1))
    out_ref[2] = scale_factor * dot_high(mine, factor_t, NN)
    out_ref[1] = factor_t

    def left_sent(n):
        drain(send.at[0], left_in.at[pl.ds(0, n)])

    if left_owners == n_dev:
        left_sent(n_dev - 1)
        drain(send.at[1], left_in.at[pl.ds(0, n_dev - 1)])
    else:
        @pl.when(me < left_owners)
        def _():
            left_sent(left_owners - 1)
            drain(send.at[1], left_in.at[pl.ds(0, n_dev - 1)])

        @pl.when(me >= left_owners)
        def _():
            left_sent(left_owners)

    drain(send.at[2], grad_in.at[pl.ds(0, n_line - 1)])
    for first, last, k in ((0, PAIR_CUT, 6), (PAIR_CUT, UNIT, 7)):
        if first < last:
            drain(send.at[k], pair_in.at[:, span(first, last), :])

    def right_sent():
        drain(send.at[4], right_in.at[pl.ds(0, n_rep - 1)])
        drain(send.at[5], sq_in.at[pl.ds(0, n_dev - 1)])

    if right_owners == n_rep:
        drain(send.at[3], right_in.at[pl.ds(0, n_rep - 1)])
        right_sent()
    else:
        @pl.when(rep < right_owners)
        def _():
            drain(send.at[3], right_in.at[pl.ds(0, right_owners - 1)])
            right_sent()

        @pl.when(rep >= right_owners)
        def _():
            drain(send.at[3], right_in.at[pl.ds(0, right_owners)])


def body(n_rep, n_shard, inputs, cotangent, momentum, right_prev):
    out_total = cotangent.shape[1]
    rows, feats = momentum.shape
    rank = right_prev.shape[1]
    n_dev = n_rep * n_shard
    scale_factor = (out_total * feats * n_shard / rank) ** 0.5
    share = max(SUB, LANE // n_rep)
    assert 2 * rank == LANE and feats == 2 * LANE and n_rep % 2 == 0
    vmem = pl.BlockSpec(memory_space=pltpu.VMEM)
    results = pl.pallas_call(
        functools.partial(kernel, n_rep, n_shard, scale_factor),
        out_shape=pltpu.VMEM((3, rows, feats), F32),
        in_specs=[pl.BlockSpec(memory_space=pltpu.HBM)] * 4,
        out_specs=vmem,
        scratch_shapes=[
            pltpu.VMEM((rank, out_total), F32),
            pltpu.VMEM((n_dev, SUB, LANE), F32),
            pltpu.VMEM((rank, out_total), F32),
            pltpu.VMEM((LANE, LANE), F32),
            pltpu.VMEM((n_rep, share, LANE), F32),
            pltpu.VMEM((LANE, LANE), F32),
            pltpu.VMEM((n_dev, 1, LANE), F32),
            pltpu.VMEM((2, n_rep // 2, rows, feats), F32),
            pltpu.VMEM((n_rep // 2, rows, feats), F32),
            pltpu.VMEM((n_rep // 2, rows, feats), F32),
            pltpu.VMEM((n_rep // 2, rows, feats), F32),
            pltpu.VMEM((LANE, feats), F32),
            pltpu.VMEM((LANE, rank), F32),
            pltpu.VMEM(inputs.shape, BF16),
            pltpu.VMEM(cotangent.shape, BF16),
            pltpu.VMEM(momentum.shape, F32),
            pltpu.VMEM((rank, feats), F32),
            pltpu.SemaphoreType.DMA((8,)),
            pltpu.SemaphoreType.DMA((8,)),
            pltpu.SemaphoreType.DMA((4,)),
        ],
        compiler_params=pltpu.CompilerParams(
            collective_id=0, has_side_effects=True, vmem_limit_bytes=60000000
        ),
    )(inputs, cotangent, momentum, right_prev.T)
    return results[0], results[1].T, results[2].astype(BF16)


def solution(mesh):
    return jax.shard_map(
        functools.partial(body, mesh.shape["rep"], mesh.shape["shard"]),
        mesh=mesh,
        in_specs=(P("rep", "shard"), P("rep", None), P("rep", "shard"), P("shard", None)),
        out_specs=(P("rep", "shard"), P("shard", None), P("rep", "shard")),
        check_vma=False,
    )
```

```python
import functools

import jax
import jax.numpy as jnp
from jax import lax
from jax.experimental import pallas as pl
from jax.experimental.pallas import tpu as pltpu
from jax.sharding import PartitionSpec as P

MESH = pl.DeviceIdType.MESH
F32, BF16 = jnp.float32, jnp.bfloat16
SUB, LANE = 8, 128
UNIT, PAIR_CUT, LINE_CUTS = 8, 4, (0, 6)
NT = (((1,), (1,)), ((), ()))
NN = (((1,), (0,)), ((), ()))
TN = (((0,), (0,)), ((), ()))


def split(x):
    hi = x.astype(BF16)
    rest = x - hi.astype(F32)
    mid = rest.astype(BF16)
    low = (rest - mid.astype(F32)).astype(BF16)
    return jnp.concatenate([hi, mid, low], axis=0)


def fold(both):
    rows = both.shape[0] // 3
    return both[:rows] + (both[rows : 2 * rows] + both[2 * rows :])


def dot_split(x, y, dims):
    return fold(lax.dot_general(split(x), y, dims, preferred_element_type=F32))


def dot_high(x, y, dims):
    return lax.dot_general(x, y, dims, precision=lax.Precision.HIGHEST, preferred_element_type=F32)


def inverse_factor(gram):
    size = gram.shape[0]
    row_at = lax.broadcasted_iota(jnp.int32, (size, size), 0)
    col_at = lax.broadcasted_iota(jnp.int32, (size, size), 1)
    eye = jnp.where(row_at == col_at, 1.0, 0.0).astype(F32)
    aug = jnp.concatenate([gram, eye], axis=1)
    width = 2 * size
    count = size // SUB
    blocks = [aug[SUB * i : SUB * (i + 1)] for i in range(count)]
    inner = lax.broadcasted_iota(jnp.int32, (SUB, width), 0)
    outs = []
    for b in range(count):
        cols = [
            [jnp.broadcast_to(blocks[i][:, SUB * b + k : SUB * b + k + 1], (SUB, width)) for i in range(b, count)]
            for k in range(SUB)
        ]
        top = blocks[b]
        scale = jnp.zeros((SUB, width), F32)
        rest = blocks[b + 1 :]
        for k in range(SUB):
            pivot = jnp.broadcast_to(cols[k][0][k : k + 1], (SUB, width))
            inv = 1.0 / pivot
            scale = jnp.where(inner == k, lax.rsqrt(pivot), scale)
            factors = [jnp.where(inner > k, cols[k][0], 0.0)] + cols[k][1:]
            for l in range(k + 1, SUB):
                mult = jnp.broadcast_to(cols[l][0][k : k + 1], (SUB, width)) * inv
                cols[l] = [c - f * mult for c, f in zip(cols[l], factors)]
            row = jnp.broadcast_to(top[k : k + 1], (SUB, width)) * inv
            top = top - factors[0] * row
            rest = [r - f * row for r, f in zip(rest, factors[1:])]
        outs.append((top * scale)[:, size:])
        blocks = blocks[: b + 1] + rest
    return jnp.concatenate(outs, axis=0)


def kernel(
    n_rep, n_shard, scale_factor,
    x_hbm, c_hbm, m_hbm, q_hbm,
    out_ref,
    left_part, left_in, left, right_part, right_in, right, sq_in, grad_part, grad_in, pair_in, pair_sum, pad, turn,
    x_ref, c_ref, m_ref, q_ref, send, recv, load,
):
    rep, shard = lax.axis_index("rep"), lax.axis_index("shard")
    n_dev = n_rep * n_shard
    me = rep * n_shard + shard
    rank = q_ref.shape[0]
    out_total = c_ref.shape[1]
    rows, feats = m_ref.shape
    row_blocks = rank // SUB
    left_owners = row_blocks * (out_total // LANE)
    share = max(SUB, LANE // n_rep)
    right_owners = LANE // share
    chunk = min(512, out_total)
    n_chunk = out_total // chunk
    per_tile = LANE // rows

    def device(index):
        return (index // n_shard, lax.rem(index, n_shard))

    def guarded(owners, total, index, fn):
        if owners == total:
            fn()
        else:
            pl.when(index < owners)(fn)

    def over(count, fn):
        if count == 1:
            fn(0)
        else:
            lax.fori_loop(0, count, lambda i, u: (fn(i), u)[1], 0)

    def lanes(i):
        if isinstance(i, int):
            return pl.ds(i * chunk, chunk)
        return pl.ds(pl.multiple_of(i * chunk, chunk), chunk)

    def copy(src, dst, k, target):
        return pltpu.make_async_remote_copy(
            src_ref=src, dst_ref=dst, send_sem=send.at[k], recv_sem=recv.at[k],
            device_id=target, device_id_type=MESH,
        )

    def drain(sem, ref):
        pltpu.make_async_copy(ref, ref, sem).wait()

    def tile(ref, t):
        r = pl.multiple_of(lax.rem(t, row_blocks) * SUB, SUB)
        c = pl.multiple_of((t // row_blocks) * LANE, LANE)
        return ref.at[pl.ds(r, SUB), pl.ds(c, LANE)]

    def band(b):
        return pl.ds(pl.multiple_of(b * share, SUB), share)

    loads = [
        pltpu.make_async_copy(src, dst, load.at[i])
        for i, (src, dst) in enumerate(((q_hbm, q_ref), (x_hbm, x_ref), (m_hbm, m_ref), (c_hbm, c_ref)))
    ]
    for each in loads:
        each.start()

    barrier = pltpu.get_barrier_semaphore()

    def greet(p, u):
        pl.semaphore_signal(barrier, inc=1, device_id=device(lax.rem(me + p, n_dev)), device_id_type=MESH)
        return u

    lax.fori_loop(1, n_dev, greet, 0)

    loads[0].wait()
    loads[1].wait()
    x = x_ref[...]
    q_t = q_ref[...]
    w_t = dot_split(q_t, x, NT)
    w_terms = split(w_t)
    loads[2].wait()
    loads[3].wait()

    def left_chunk(i):
        both = lax.dot_general(w_terms, c_ref[:, lanes(i)], NN, preferred_element_type=F32)
        left_part[:, lanes(i)] = fold(both)

    over(n_chunk, left_chunk)
    pad[...] = jnp.zeros_like(pad)
    half = lax.rem(rep, per_tile)
    my_rows = pl.ds(pl.multiple_of(half * rows, rows), rows)
    my_lanes = pl.ds(pl.multiple_of((rep // per_tile) * LANE, LANE), LANE)
    pad[my_rows, :] = m_ref[...]
    left_part[:, my_lanes] += dot_high(q_t, pad[...], NT)

    pl.semaphore_wait(barrier, n_dev - 1)

    def send_left(p, u):
        t = lax.rem(me + p, n_dev)
        guarded(left_owners, n_dev, t, lambda: copy(tile(left_part, t), left_in.at[me], 0, device(t)).start())
        return u

    lax.fori_loop(1, n_dev, send_left, 0)

    n_line = n_rep // 2
    line, side = rep // 2, lax.rem(rep, 2)
    unit = rows // UNIT

    def span(first, last):
        return pl.ds(first * unit, (last - first) * unit)

    def send_pair(first, last, k):
        if first == last:
            return
        part = span(first, last)
        copy(
            grad_part.at[1 - side, :, part, :], pair_in.at[:, part, :], k, (2 * line + 1 - side, shard)
        ).start()

    def take_pair(first, last, k):
        if first == last:
            return
        part = span(first, last)
        drain(recv.at[k], pair_in.at[:, part, :])
        for h in range(n_line) if n_line <= 8 else ():
            pair_sum[h, part, :] = grad_part[side, h, part, :] + pair_in[h, part, :]
        if n_line > 8:
            def add(h, u):
                pair_sum[h, part, :] = grad_part[side, h, part, :] + pair_in[h, part, :]
                return u

            lax.fori_loop(0, n_line, add, 0)

    def send_line(first, last):
        if first == last:
            return
        part = span(first, last)

        def one(p, u):
            t = lax.rem(line + p, n_line)
            copy(pair_sum.at[t, part, :], grad_in.at[line, part, :], 2, (2 * t + side, shard)).start()
            return u

        lax.fori_loop(1, n_line, one, 0)

    def grad_chunk(i):
        g = lax.dot_general(c_ref[:, lanes(i)], x, TN, preferred_element_type=F32)
        for r in range(chunk // rows):
            at = i * (chunk // rows) + r
            grad_part[at % 2, at // 2] = g[r * rows : (r + 1) * rows]

    over(n_chunk, grad_chunk)
    send_pair(0, PAIR_CUT, 6)

    def own_left():
        left_in[me] = tile(left_part, me)[...]
        drain(recv.at[0], left_in.at[pl.ds(0, n_dev - 1)])
        tile(left, me)[...] = jnp.sum(left_in[...], axis=0)

        def give(p, u):
            copy(tile(left, me), tile(left, me), 1, device(lax.rem(me + p, n_dev))).start()
            return u

        lax.fori_loop(1, n_dev, give, 0)

    guarded(left_owners, n_dev, me, own_left)

    send_pair(PAIR_CUT, UNIT, 7)
    if left_owners == n_dev:
        drain(recv.at[1], left_in.at[pl.ds(0, n_dev - 1)])
    else:
        @pl.when(me < left_owners)
        def _():
            drain(recv.at[1], left_in.at[pl.ds(0, left_owners - 1)])

        @pl.when(me >= left_owners)
        def _():
            drain(recv.at[1], left_in.at[pl.ds(0, left_owners)])


    if n_chunk == 1:
        v_t = dot_split(left[...], c_ref[...], NT)
    else:
        v_t = lax.fori_loop(
            0, n_chunk,
            lambda i, v: v + dot_split(left[:, lanes(i)], c_ref[:, lanes(i)], NT),
            jnp.zeros((rank, c_ref.shape[0]), F32),
        )
    mine_t = left[:, my_lanes]
    cross_t = dot_split(v_t, x, NN) + dot_high(mine_t, pad[...], NN)
    right_part[...] = jnp.concatenate([cross_t[:, :LANE], cross_t[:, LANE:]], axis=0).T

    def send_right(p, u):
        t = lax.rem(rep + p, n_rep)
        guarded(
            right_owners, n_rep, t,
            lambda: copy(right_part.at[band(t), :], right_in.at[rep], 3, (t, shard)).start(),
        )
        return u

    lax.fori_loop(1, n_rep, send_right, 0)
    take_pair(0, PAIR_CUT, 6)
    take_pair(PAIR_CUT, UNIT, 7)
    send_line(LINE_CUTS[0], LINE_CUTS[1])

    if n_chunk == 1:
        whole = left[...]
        gram = dot_high(whole, whole, NT)
    else:
        gram = lax.fori_loop(
            0, n_chunk,
            lambda i, g: g + dot_high(left[:, lanes(i)], left[:, lanes(i)], NT),
            jnp.zeros((rank, rank), F32),
        )
    inv = inverse_factor(gram)
    turn[...] = mine_t.T
    mine = dot_high(turn[my_rows, :], inv, NT)
    none = jnp.zeros((rank, rank), F32)
    inv_two = jnp.concatenate(
        [jnp.concatenate([inv, none], axis=1), jnp.concatenate([none, inv], axis=1)], axis=0
    )

    def own_right():
        right_in[rep] = right_part[band(rep), :]
        drain(recv.at[3], right_in.at[pl.ds(0, n_rep - 1)])
        total = dot_high(jnp.sum(right_in[...], axis=0), inv_two, NT)
        right[band(rep), :] = total
        sq_in[me] = jnp.sum(total * total, axis=0, keepdims=True)

        def give_right(p, u):
            copy(right.at[band(rep), :], right.at[band(rep), :], 4, (lax.rem(rep + p, n_rep), shard)).start()
            return u

        lax.fori_loop(1, n_rep, give_right, 0)

        def give_sq(p, u):
            copy(sq_in.at[me], sq_in.at[me], 5, device(lax.rem(me + p, n_dev))).start()
            return u

        lax.fori_loop(1, n_dev, give_sq, 0)

    guarded(right_owners, n_rep, rep, own_right)

    send_line(LINE_CUTS[1], UNIT)

    grad_in[line] = pair_sum[line]
    drain(recv.at[2], grad_in.at[pl.ds(0, n_line - 1)])
    blended = m_ref[...] + lax.fori_loop(1, n_line, lambda r, g: g + grad_in[r], grad_in[0])

    def finish_recv(n_right, n_sq):
        drain(recv.at[4], right_in.at[pl.ds(0, n_right)])
        flat = sq_in.at[pl.ds(0, n_sq)]
        drain(recv.at[5], flat)

    sq_all = right_owners * n_shard
    if right_owners == n_rep:
        finish_recv(right_owners - 1, sq_all - 1)
    else:
        @pl.when(rep < right_owners)
        def _():
            finish_recv(right_owners - 1, sq_all - 1)

        @pl.when(rep >= right_owners)
        def _():
            finish_recv(right_owners, sq_all)

    def wide(packed):
        t = packed.T
        return jnp.concatenate([t[:rank], t[rank:]], axis=1)

    packed = right[...]
    right_t = wide(packed)
    out_ref[0] = blended - 0.05 * dot_high(mine, right_t, NN)
    halves = jnp.sum(sq_in[pl.ds(0, sq_all)], axis=0)
    column_sq = halves[:, :rank] + halves[:, rank:]
    norm = jnp.sqrt(column_sq + 1e-06)
    factor_t = wide(packed / jnp.concatenate([norm, norm], axis=1))
    out_ref[2] = scale_factor * dot_high(mine, factor_t, NN)
    out_ref[1] = factor_t

    def left_sent(n):
        drain(send.at[0], left_in.at[pl.ds(0, n)])

    if left_owners == n_dev:
        left_sent(n_dev - 1)
        drain(send.at[1], left_in.at[pl.ds(0, n_dev - 1)])
    else:
        @pl.when(me < left_owners)
        def _():
            left_sent(left_owners - 1)
            drain(send.at[1], left_in.at[pl.ds(0, n_dev - 1)])

        @pl.when(me >= left_owners)
        def _():
            left_sent(left_owners)

    drain(send.at[2], grad_in.at[pl.ds(0, n_line - 1)])
    for first, last, k in ((0, PAIR_CUT, 6), (PAIR_CUT, UNIT, 7)):
        if first < last:
            drain(send.at[k], pair_in.at[:, span(first, last), :])

    def right_sent():
        drain(send.at[4], right_in.at[pl.ds(0, n_rep - 1)])
        drain(send.at[5], sq_in.at[pl.ds(0, n_dev - 1)])

    if right_owners == n_rep:
        drain(send.at[3], right_in.at[pl.ds(0, n_rep - 1)])
        right_sent()
    else:
        @pl.when(rep < right_owners)
        def _():
            drain(send.at[3], right_in.at[pl.ds(0, right_owners - 1)])
            right_sent()

        @pl.when(rep >= right_owners)
        def _():
            drain(send.at[3], right_in.at[pl.ds(0, right_owners)])


def body(n_rep, n_shard, inputs, cotangent, momentum, right_prev):
    out_total = cotangent.shape[1]
    rows, feats = momentum.shape
    rank = right_prev.shape[1]
    n_dev = n_rep * n_shard
    scale_factor = (out_total * feats * n_shard / rank) ** 0.5
    share = max(SUB, LANE // n_rep)
    assert 2 * rank == LANE and feats == 2 * LANE and n_rep % 2 == 0
    vmem = pl.BlockSpec(memory_space=pltpu.VMEM)
    results = pl.pallas_call(
        functools.partial(kernel, n_rep, n_shard, scale_factor),
        out_shape=pltpu.VMEM((3, rows, feats), F32),
        in_specs=[pl.BlockSpec(memory_space=pltpu.HBM)] * 4,
        out_specs=vmem,
        scratch_shapes=[
            pltpu.VMEM((rank, out_total), F32),
            pltpu.VMEM((n_dev, SUB, LANE), F32),
            pltpu.VMEM((rank, out_total), F32),
            pltpu.VMEM((LANE, LANE), F32),
            pltpu.VMEM((n_rep, share, LANE), F32),
            pltpu.VMEM((LANE, LANE), F32),
            pltpu.VMEM((n_dev, 1, LANE), F32),
            pltpu.VMEM((2, n_rep // 2, rows, feats), F32),
            pltpu.VMEM((n_rep // 2, rows, feats), F32),
            pltpu.VMEM((n_rep // 2, rows, feats), F32),
            pltpu.VMEM((n_rep // 2, rows, feats), F32),
            pltpu.VMEM((LANE, feats), F32),
            pltpu.VMEM((LANE, rank), F32),
            pltpu.VMEM(inputs.shape, BF16),
            pltpu.VMEM(cotangent.shape, BF16),
            pltpu.VMEM(momentum.shape, F32),
            pltpu.VMEM((rank, feats), F32),
            pltpu.SemaphoreType.DMA((8,)),
            pltpu.SemaphoreType.DMA((8,)),
            pltpu.SemaphoreType.DMA((4,)),
        ],
        compiler_params=pltpu.CompilerParams(
            collective_id=0, has_side_effects=True, vmem_limit_bytes=60000000
        ),
    )(inputs, cotangent, momentum, right_prev.T)
    return results[0], results[1].T, results[2].astype(BF16)


def solution(mesh):
    return jax.shard_map(
        functools.partial(body, mesh.shape["rep"], mesh.shape["shard"]),
        mesh=mesh,
        in_specs=(P("rep", "shard"), P("rep", None), P("rep", "shard"), P("shard", None)),
        out_specs=(P("rep", "shard"), P("shard", None), P("rep", "shard")),
        check_vma=False,
    )
```
